256 devices in a mesh: row: 8 (over y, x_lo), col: 32 (over x_hi, z, core).
Axes of the slice: x: 4 (x_hi: 2, x_lo: 2; x = x_hi * 2 + x_lo), y: 4, z: 8, core: 2. Of those that a mesh axis runs over, the one named last changes fastest.
Arguments:
- density: float32 [4096, 4096], P('row', 'col'), as said below
- pattern: int32 [32, 6], replicated, may hold values from 0 to 31, as said below
Outputs:
- purified: float32 [4096, 4096], P('row', 'col')
The draws below stay inside these ranges and needn't reach their ends.
Inputs may be any that keep to these rules, and one draw needn't show every extreme that they name: density is symmetric. `pattern`: each row lists 6 different block columns; the first is the row's own index.
All inputs are finite; a program needn't handle non-finite values.
Results may differ from the reference program's by a relative error of at most 0.00021.
Values sent between devices are 32-bit elements; how exact they have to be, the bound alone decides.
No kernel may reach another device: no remote copies, remote signals or barrier semaphores. Data moves between devices by JAX's collectives and lax.ppermute only.
A program may use at most 64 MiB of HBM per device.

```python
import jax
import jax.numpy as jnp
from jax import lax

BLK = 128
NNZ = 6
ITERS = 2
BLOCKS_PER_SIDE = 32
ORDER = 4096


def draw_pattern(key, part):
    key_rank, key_noise = jax.random.split(jax.random.fold_in(key, 11))
    column_position = jax.random.permutation(key_rank, BLOCKS_PER_SIDE).astype(jnp.int32)
    random_noise_term = jax.random.randint(key_noise, (BLOCKS_PER_SIDE, BLOCKS_PER_SIDE), 0, 4096, dtype=jnp.int32)
    row_index_list = jnp.arange(BLOCKS_PER_SIDE, dtype=jnp.int32)
    diagonal_boost = jnp.where(row_index_list[:, None] == row_index_list[None, :], 1048576, 0).astype(jnp.int32)
    block_ranking = (random_noise_term + column_position[None, :] * (4096 // BLOCKS_PER_SIDE) + diagonal_boost) * BLOCKS_PER_SIDE + row_index_list[None, :]
    return lax.top_k(block_ranking, NNZ)[1].astype(jnp.int32)


def draw_density(key, part):
    key_base = jax.random.fold_in(jax.random.fold_in(key, 23), 0)
    base = jax.random.normal(key_base, (ORDER, ORDER), jnp.float32)
    return jnp.clip((base + base.T) * 0.70710678, -6.0, 6.0).astype(jnp.float32)


def setup_inputs(seed: int = 0) -> dict:
    key_of = jax.random.split(jax.random.key(seed), 3)
    return {
        "density": draw_density(jax.random.fold_in(key_of[2], 71), 0),
        "pattern": draw_pattern(jax.random.fold_in(key_of[2], 71), 0),
    }


def full_product(left, right):
    return jnp.dot(left, right, precision=lax.Precision.HIGHEST, preferred_element_type=jnp.float32)

def reference(density, pattern):
    block_count = pattern.shape[0]
    matrix_order = density.shape[0]
    listed = jnp.any(pattern[:, :, None] == jnp.arange(block_count, dtype=jnp.int32)[None, None, :], axis=1).astype(jnp.float32)
    block_live = jnp.maximum(listed, listed.T)
    pattern_mask = jnp.repeat(jnp.repeat(block_live, BLK, axis=0), BLK, axis=1)
    identity = jnp.eye(matrix_order, dtype=jnp.float32)
    current = 0.5 * identity + 0.45 / jnp.sqrt(jnp.float32(2 * NNZ * BLK)) * pattern_mask * density
    for purify_round in range(ITERS):
        square = pattern_mask * full_product(current, current)
        cube = pattern_mask * full_product(current, square)
        current = 3.0 * square - 2.0 * cube
    return current
```

```python
import jax
import jax.numpy as jnp
from jax import lax
from jax.sharding import PartitionSpec as P

BLK = 128
NNZ = 6
ITERS = 2


def product(left, right):
    return jnp.dot(left, right, precision=lax.Precision.HIGH, preferred_element_type=jnp.float32)


def gather_rows(tile, name):
    parts = lax.axis_size(name)
    copies = jnp.broadcast_to(tile[None], (parts,) + tile.shape)
    got = lax.all_to_all(copies, name, 0, 0)
    return got.reshape(parts * tile.shape[0], tile.shape[1])


def local(density, pattern):
    rows_dev, cols_dev = density.shape
    row_number = lax.axis_index("row")
    col_index = lax.axis_index("col")
    matrix_order = cols_dev * lax.axis_size("col")
    block_count = matrix_order // BLK
    tile_blocks = cols_dev // BLK
    row_blocks = rows_dev // BLK
    listed = jnp.any(
        pattern[:, :, None] == jnp.arange(block_count, dtype=jnp.int32)[None, None, :], axis=1
    ).astype(jnp.float32)
    block_live = jnp.maximum(listed, listed.T)
    my_rows = lax.dynamic_slice_in_dim(block_live, row_number * row_blocks, row_blocks, 0)
    own_blocks = lax.dynamic_slice_in_dim(my_rows, col_index * tile_blocks, tile_blocks, 1)
    pattern_mask = jnp.repeat(jnp.repeat(own_blocks, BLK, axis=0), BLK, axis=1)
    global_rows = row_number * rows_dev + jnp.arange(rows_dev, dtype=jnp.int32)
    global_cols = col_index * cols_dev + jnp.arange(cols_dev, dtype=jnp.int32)
    identity = (global_rows[:, None] == global_cols[None, :]).astype(jnp.float32)
    current = 0.5 * identity + 0.45 / jnp.sqrt(jnp.float32(2 * NNZ * BLK)) * pattern_mask * density
    for purify_round in range(ITERS):
        row_panel = lax.all_gather(current, "col", axis=1, tiled=True)
        column_panel = gather_rows(current, "row")
        square = pattern_mask * product(row_panel, column_panel)
        square_panel = gather_rows(square, "row")
        cube = pattern_mask * product(row_panel, square_panel)
        current = 3.0 * square - 2.0 * cube
    return current


def solution(mesh):
    return jax.shard_map(
        local,
        mesh=mesh,
        in_specs=(P("row", "col"), P()),
        out_specs=P("row", "col"),
        check_vma=False,
    )
```

```python
import jax
import jax.numpy as jnp
from jax import lax
from jax.experimental import pallas as pl
from jax.experimental.pallas import tpu as pltpu
from jax.sharding import PartitionSpec as P

BLK = 128
NNZ = 6
ITERS = 2
X_HI, Z, CORE = 2, 8, 2
GROUP = 4


def gather_rows(tile, name):
    parts = lax.axis_size(name)
    copies = jnp.broadcast_to(tile[None], (parts,) + tile.shape)
    got = lax.all_to_all(copies, name, 0, 0)
    return got.reshape(parts * tile.shape[0], tile.shape[1])


def col_id(x_hi, z, core):
    return (x_hi * Z + z % Z) * CORE + core


COLS = [(x, z, c) for x in range(X_HI) for z in range(Z) for c in range(CORE)]
UP = [(col_id(x, z, c), col_id(x, z + 1, c)) for x, z, c in COLS]
DOWN = [(col_id(x, z, c), col_id(x, z - 1, c)) for x, z, c in COLS]
ACROSS = [(col_id(x, z, c), col_id(1 - x, z, c)) for x, z, c in COLS]
TWIN = [(col_id(x, z, c), col_id(x, z, 1 - c)) for x, z, c in COLS]


def gather_cols(tile):
    send = lambda v, pairs: lax.ppermute(v, "col", pairs)
    both = jnp.stack([tile, send(tile, ACROSS)])
    up = down = both
    pieces = [both]
    for _ in range(3):
        up, down = send(up, UP), send(down, DOWN)
        pieces += [up, down]
    pieces += [send(up[:1], UP), send(down[1:], DOWN)]
    return pieces + [send(p, TWIN) for p in pieces]


def piece_columns(col):
    x_hi, z, core = col // (Z * CORE), (col // CORE) % Z, col % CORE
    out = []
    for c in (core, 1 - core):
        for d in (0, -1, 1, -2, 2, -3, 3):
            out += [col_id(x_hi, z + d + Z, c), col_id(1 - x_hi, z + d + Z, c)]
        out += [col_id(x_hi, z + 4, c), col_id(1 - x_hi, z + 4, c)]
    return jnp.stack(out).astype(jnp.int32)


def split(x):
    high = x.astype(jnp.bfloat16)
    return high, (x - high.astype(jnp.float32)).astype(jnp.bfloat16)


def product_body(sizes, combine, columns, live, *refs):
    pieces = refs[: len(sizes)]
    panel = refs[len(sizes)]
    square = refs[len(sizes) + 1] if combine else None
    out, held, total, sems = refs[-4:]
    slot = 0
    for piece, n in zip(pieces, sizes):
        for j in range(n):
            pltpu.make_async_copy(piece.at[j], held.at[slot], sems.at[slot]).start()
            slot += 1
    total[...] = jnp.zeros_like(total)

    def step(g, carry):
        left, right = [], []
        for q in range(GROUP):
            s = g * GROUP + q
            pltpu.make_async_copy(held.at[s], held.at[s], sems.at[s]).wait()
            left.append(held[s])
            right.append(panel[pl.ds(pl.multiple_of(columns[s] * BLK, BLK), BLK), :])
        left_high, left_low = split(jnp.concatenate(left, axis=1))
        right_high, right_low = split(jnp.concatenate(right, axis=0))
        wide = jnp.dot(
            left_high,
            jnp.concatenate([right_high, right_low], axis=1),
            preferred_element_type=jnp.float32,
        )
        narrow = jnp.dot(left_low, right_high, preferred_element_type=jnp.float32)
        total[...] += (wide[:, BLK:] + narrow) + wide[:, :BLK]
        return carry

    lax.fori_loop(0, held.shape[0] // GROUP, step, 0)
    for i in range(out.shape[0] // BLK):
        rows = pl.ds(i * BLK, BLK)
        masked = live[i] * total[rows, :]
        out[rows, :] = 3.0 * square[rows, :] - 2.0 * masked if combine else masked


def product(columns, live, pieces, panel, square=None):
    rows = pieces[0].shape[1]
    sizes = [p.shape[0] for p in pieces]
    slots = sum(sizes)
    smem = pl.BlockSpec(memory_space=pltpu.SMEM)
    vmem = pl.BlockSpec(memory_space=pltpu.VMEM)
    combine = square is not None
    body = lambda *refs: product_body(sizes, combine, *refs)
    return pl.pallas_call(
        body,
        out_shape=jax.ShapeDtypeStruct((rows, BLK), jnp.float32),
        in_specs=[smem, smem]
        + [pl.BlockSpec(memory_space=pl.ANY)] * len(pieces)
        + [vmem] * (2 if combine else 1),
        out_specs=vmem,
        scratch_shapes=[
            pltpu.VMEM((slots, rows, BLK), jnp.float32),
            pltpu.VMEM((rows, BLK), jnp.float32),
            pltpu.SemaphoreType.DMA((slots,)),
        ],
        compiler_params=pltpu.CompilerParams(vmem_limit_bytes=32 << 20),
        cost_estimate=pl.CostEstimate(
            flops=6 * rows * slots * BLK * BLK,
            bytes_accessed=4 * BLK * (slots * (rows + BLK) + 2 * rows),
            transcendentals=0,
        ),
    )(columns, live, *pieces, panel, *([square] if combine else []))


def local(density, pattern):
    rows_dev, cols_dev = density.shape
    row_number = lax.axis_index("row")
    col_index = lax.axis_index("col")
    matrix_order = cols_dev * lax.axis_size("col")
    block_count = matrix_order // BLK
    row_blocks = rows_dev // BLK
    listed = jnp.any(
        pattern[:, :, None] == jnp.arange(block_count, dtype=jnp.int32)[None, None, :], axis=1
    ).astype(jnp.float32)
    block_live = jnp.maximum(listed, listed.T)
    my_rows = lax.dynamic_slice_in_dim(block_live, row_number * row_blocks, row_blocks, 0)
    live = lax.dynamic_slice_in_dim(my_rows, col_index, 1, 1)[:, 0]
    pattern_mask = jnp.repeat(live, BLK)[:, None]
    global_rows = row_number * rows_dev + jnp.arange(rows_dev, dtype=jnp.int32)
    global_cols = col_index * cols_dev + jnp.arange(cols_dev, dtype=jnp.int32)
    identity = (global_rows[:, None] == global_cols[None, :]).astype(jnp.float32)
    current = 0.5 * identity + 0.45 / jnp.sqrt(jnp.float32(2 * NNZ * BLK)) * pattern_mask * density
    columns = piece_columns(col_index)
    for purify_round in range(ITERS):
        column_panel = lax.all_gather(current, "row", axis=0, tiled=True)
        pieces = gather_cols(current)
        square = product(columns, live, pieces, column_panel)
        square_panel = gather_rows(square, "row")
        current = product(columns, live, pieces, square_panel, square)
    return current


def solution(mesh):
    return jax.shard_map(
        local,
        mesh=mesh,
        in_specs=(P("row", "col"), P()),
        out_specs=P("row", "col"),
        check_vma=False,
    )
```

```python
import jax
import jax.numpy as jnp
from jax import lax
from jax.experimental import pallas as pl
from jax.experimental.pallas import tpu as pltpu
from jax.sharding import PartitionSpec as P

BLK = 128
NNZ = 6
ITERS = 2
X_HI, Z, CORE = 2, 8, 2
GROUP = 4


def gather_rows(tile, name):
    parts = lax.axis_size(name)
    copies = jnp.broadcast_to(tile[None], (parts,) + tile.shape)
    got = lax.all_to_all(copies, name, 0, 0)
    return got.reshape(parts * tile.shape[0], tile.shape[1])


def col_id(x_hi, z, core):
    return (x_hi * Z + z % Z) * CORE + core


COLS = [(x, z, c) for x in range(X_HI) for z in range(Z) for c in range(CORE)]
UP = [(col_id(x, z, c), col_id(x, z + 1, c)) for x, z, c in COLS]
DOWN = [(col_id(x, z, c), col_id(x, z - 1, c)) for x, z, c in COLS]
ACROSS = [(col_id(x, z, c), col_id(1 - x, z, c)) for x, z, c in COLS]
TWIN = [(col_id(x, z, c), col_id(x, z, 1 - c)) for x, z, c in COLS]


def gather_cols(tile):
    send = lambda v, pairs: lax.ppermute(v, "col", pairs)
    both = jnp.stack([tile, send(tile, ACROSS)])
    up = down = both
    pieces = [both]
    for _ in range(3):
        up, down = send(up, UP), send(down, DOWN)
        pieces += [up, down]
    pieces += [send(up[:1], UP), send(down[1:], DOWN)]
    return pieces + [send(p, TWIN) for p in pieces]


def piece_columns(col):
    x_hi, z, core = col // (Z * CORE), (col // CORE) % Z, col % CORE
    out = []
    for c in (core, 1 - core):
        for d in (0, -1, 1, -2, 2, -3, 3):
            out += [col_id(x_hi, z + d + Z, c), col_id(1 - x_hi, z + d + Z, c)]
        out += [col_id(x_hi, z + 4, c), col_id(1 - x_hi, z + 4, c)]
    return jnp.stack(out).astype(jnp.int32)


def split(x):
    high = x.astype(jnp.bfloat16)
    return high, (x - high.astype(jnp.float32)).astype(jnp.bfloat16)


def product_body(sizes, combine, columns, live, *refs):
    pieces = refs[: len(sizes)]
    panel = refs[len(sizes)]
    square = refs[len(sizes) + 1] if combine else None
    out, total = refs[-2:]
    slots = [(piece, j) for piece, n in zip(pieces, sizes) for j in range(n)]
    for g in range(0, len(slots), GROUP):
        left, right = [], []
        for s in range(g, g + GROUP):
            piece, j = slots[s]
            left.append(piece[j])
            right.append(panel[pl.ds(pl.multiple_of(columns[s] * BLK, BLK), BLK), :])
        left_high, left_low = split(jnp.concatenate(left, axis=1))
        right_high, right_low = split(jnp.concatenate(right, axis=0))
        wide = jnp.dot(
            left_high,
            jnp.concatenate([right_high, right_low], axis=1),
            preferred_element_type=jnp.float32,
        )
        narrow = jnp.dot(left_low, right_high, preferred_element_type=jnp.float32)
        term = (wide[:, BLK:] + narrow) + wide[:, :BLK]
        total[...] = term if g == 0 else total[...] + term
    for i in range(out.shape[0] // BLK):
        rows = pl.ds(i * BLK, BLK)
        masked = live[i] * total[rows, :]
        out[rows, :] = 3.0 * square[rows, :] - 2.0 * masked if combine else masked


def product(columns, live, pieces, panel, square=None):
    rows = pieces[0].shape[1]
    sizes = [p.shape[0] for p in pieces]
    slots = sum(sizes)
    smem = pl.BlockSpec(memory_space=pltpu.SMEM)
    vmem = pl.BlockSpec(memory_space=pltpu.VMEM)
    combine = square is not None
    body = lambda *refs: product_body(sizes, combine, *refs)
    return pl.pallas_call(
        body,
        out_shape=jax.ShapeDtypeStruct((rows, BLK), jnp.float32),
        in_specs=[smem, smem] + [vmem] * (len(pieces) + (2 if combine else 1)),
        out_specs=vmem,
        scratch_shapes=[pltpu.VMEM((rows, BLK), jnp.float32)],
        compiler_params=pltpu.CompilerParams(vmem_limit_bytes=24 << 20),
        cost_estimate=pl.CostEstimate(
            flops=6 * rows * slots * BLK * BLK,
            bytes_accessed=4 * BLK * (slots * (rows + BLK) + 2 * rows),
            transcendentals=0,
        ),
    )(columns, live, *pieces, panel, *([square] if combine else []))


def local(density, pattern):
    rows_dev, cols_dev = density.shape
    row_number = lax.axis_index("row")
    col_index = lax.axis_index("col")
    matrix_order = cols_dev * lax.axis_size("col")
    block_count = matrix_order // BLK
    row_blocks = rows_dev // BLK
    listed = jnp.any(
        pattern[:, :, None] == jnp.arange(block_count, dtype=jnp.int32)[None, None, :], axis=1
    ).astype(jnp.float32)
    block_live = jnp.maximum(listed, listed.T)
    my_rows = lax.dynamic_slice_in_dim(block_live, row_number * row_blocks, row_blocks, 0)
    live = lax.dynamic_slice_in_dim(my_rows, col_index, 1, 1)[:, 0]
    pattern_mask = jnp.repeat(live, BLK)[:, None]
    global_rows = row_number * rows_dev + jnp.arange(rows_dev, dtype=jnp.int32)
    global_cols = col_index * cols_dev + jnp.arange(cols_dev, dtype=jnp.int32)
    identity = (global_rows[:, None] == global_cols[None, :]).astype(jnp.float32)
    current = 0.5 * identity + 0.45 / jnp.sqrt(jnp.float32(2 * NNZ * BLK)) * pattern_mask * density
    columns = piece_columns(col_index)
    for purify_round in range(ITERS):
        column_panel = lax.all_gather(current, "row", axis=0, tiled=True)
        pieces = gather_cols(current)
        square = product(columns, live, pieces, column_panel)
        square_panel = gather_rows(square, "row")
        current = product(columns, live, pieces, square_panel, square)
    return current


def solution(mesh):
    return jax.shard_map(
        local,
        mesh=mesh,
        in_specs=(P("row", "col"), P()),
        out_specs=P("row", "col"),
        check_vma=False,
    )
```

```python
import jax
import jax.numpy as jnp
from jax import lax
from jax.experimental import pallas as pl
from jax.experimental.pallas import tpu as pltpu
from jax.sharding import PartitionSpec as P

BLK = 128
NNZ = 6
ITERS = 2
X_HI, Z, CORE = 2, 8, 2
GROUP = 4


def col_id(x_hi, z, core):
    return (x_hi * Z + z % Z) * CORE + core


COLS = [(x, z, c) for x in range(X_HI) for z in range(Z) for c in range(CORE)]
UP = [(col_id(x, z, c), col_id(x, z + 1, c)) for x, z, c in COLS]
DOWN = [(col_id(x, z, c), col_id(x, z - 1, c)) for x, z, c in COLS]
ACROSS = [(col_id(x, z, c), col_id(1 - x, z, c)) for x, z, c in COLS]
TWIN = [(col_id(x, z, c), col_id(x, z, 1 - c)) for x, z, c in COLS]


def send(v, pairs):
    return lax.ppermute(v, "col", pairs)


def gather_rows(tile, name):
    parts = lax.axis_size(name)
    copies = jnp.broadcast_to(tile[None], (parts,) + tile.shape)
    got = lax.all_to_all(copies, name, 0, 0)
    return got.reshape(parts * tile.shape[0], tile.shape[1])


def gather_cols(tile):
    both = jnp.stack([tile, send(tile, ACROSS)])
    up = down = both
    pieces = [both]
    for _ in range(3):
        up, down = send(up, UP), send(down, DOWN)
        pieces += [up, down]
    return pieces + [send(up[:1], UP), send(down[1:], DOWN)]


def piece_columns(col):
    x_hi, z, core = col // (Z * CORE), (col // CORE) % Z, col % CORE
    away = jnp.array([0, 0, -1, -1, 1, 1, -2, -2, 2, 2, -3, -3, 3, 3, 4, 4], jnp.int32)
    across = jnp.arange(X_HI * Z, dtype=jnp.int32) % X_HI
    places = (x_hi + across) % X_HI * Z + (z + away + Z) % Z
    return jnp.concatenate([places, core[None].astype(jnp.int32)])


def to_pair(tile, core):
    rows = tile.reshape(-1, CORE, BLK, BLK)
    mine = jnp.where(core == 0, rows[:, 0], rows[:, 1])
    other = send(jnp.where(core == 0, rows[:, 1], rows[:, 0]), TWIN)
    left = jnp.where(core == 0, mine, other)
    right = jnp.where(core == 0, other, mine)
    return jnp.concatenate([left, right], axis=2).reshape(-1, CORE * BLK)


def split(x):
    high = x.astype(jnp.bfloat16)
    return high, (x - high.astype(jnp.float32)).astype(jnp.bfloat16)


def partial_product(sizes, where, pieces, panel, total):
    slots = [(piece, j) for piece, n in zip(pieces, sizes) for j in range(n)]
    for g in range(0, len(slots), GROUP):
        left, right = [], []
        for s in range(g, g + GROUP):
            piece, j = slots[s]
            left.append(piece[j])
            right.append(panel[pl.ds(pl.multiple_of(where[s] * BLK, BLK), BLK), :])
        left_high, left_low = split(jnp.concatenate(left, axis=1))
        right_high, right_low = split(jnp.concatenate(right, axis=0))
        dot = lambda a, b: jnp.dot(a, b, preferred_element_type=jnp.float32)
        term = (dot(left_high, right_low) + dot(left_low, right_high)) + dot(left_high, right_high)
        total[...] = term if g == 0 else total[...] + term


def mask_pair(block, live, i):
    return jnp.concatenate(
        [live[CORE * i + c] * block[:, c * BLK : (c + 1) * BLK] for c in range(CORE)], axis=1
    )


def square_body(sizes, where, live, *refs):
    *pieces, panel, keep, give, total = refs
    partial_product(sizes, where, pieces, panel, total)
    core = where[sum(sizes)]
    for q in range(keep.shape[0] // BLK):
        for out, i in ((keep, CORE * q + core), (give, CORE * q + 1 - core)):
            block = total[pl.ds(pl.multiple_of(i * BLK, BLK), BLK), :]
            out[pl.ds(q * BLK, BLK), :] = mask_pair(block, live, i)


def step_body(sizes, where, live, *refs):
    *pieces, panel, kept, given, keep, give, total = refs
    partial_product(sizes, where, pieces, panel, total)
    core = where[sum(sizes)]
    first = core == 0
    for i in range(keep.shape[0] // BLK):
        rows = pl.ds(i * BLK, BLK)
        q = pl.ds(i // CORE * BLK, BLK)
        square = jnp.where(core == i % CORE, kept[q, :], given[q, :])
        part = 3.0 * square - 2.0 * mask_pair(total[rows, :], live, i)
        keep[rows, :] = jnp.where(first, part[:, :BLK], part[:, BLK:])
        give[rows, :] = jnp.where(first, part[:, BLK:], part[:, :BLK])


def call(body, where, live, pieces, panel, extra, shape):
    rows = pieces[0].shape[1]
    sizes = [p.shape[0] for p in pieces]
    slots = sum(sizes)
    width = panel.shape[1]
    vmem = pl.BlockSpec(memory_space=pltpu.VMEM)
    out = jax.ShapeDtypeStruct(shape, jnp.float32)
    return pl.pallas_call(
        lambda *refs: body(sizes, *refs),
        out_shape=(out, out),
        in_specs=[pl.BlockSpec(memory_space=pltpu.SMEM)] * 2 + [vmem] * (len(pieces) + 1 + len(extra)),
        out_specs=(vmem, vmem),
        scratch_shapes=[pltpu.VMEM((rows, width), jnp.float32)],
        compiler_params=pltpu.CompilerParams(vmem_limit_bytes=16 << 20),
        cost_estimate=pl.CostEstimate(
            flops=6 * rows * slots * BLK * width,
            bytes_accessed=4 * (slots * BLK * (rows + width) + 2 * rows * width),
            transcendentals=0,
        ),
    )(where, live, *pieces, panel, *extra)


def local(density, pattern):
    rows_dev, cols_dev = density.shape
    row_number = lax.axis_index("row")
    col_index = lax.axis_index("col")
    core = col_index % CORE
    block_count = cols_dev * lax.axis_size("col") // BLK
    row_blocks = rows_dev // BLK
    listed = jnp.any(
        pattern[:, :, None] == jnp.arange(block_count, dtype=jnp.int32)[None, None, :], axis=1
    ).astype(jnp.float32)
    block_live = jnp.maximum(listed, listed.T)
    my_rows = lax.dynamic_slice_in_dim(block_live, row_number * row_blocks, row_blocks, 0)
    chip = lax.dynamic_slice_in_dim(my_rows, col_index - core, CORE, 1)
    tile_live = jnp.where(core == 0, chip[:, 0], chip[:, 1])
    tile_mask = jnp.repeat(tile_live, BLK)[:, None]
    live = chip.reshape(-1)
    global_rows = row_number * rows_dev + jnp.arange(rows_dev, dtype=jnp.int32)
    global_cols = col_index * cols_dev + jnp.arange(cols_dev, dtype=jnp.int32)
    identity = (global_rows[:, None] == global_cols[None, :]).astype(jnp.float32)
    current = 0.5 * identity + 0.45 / jnp.sqrt(jnp.float32(2 * NNZ * BLK)) * tile_mask * density
    where = piece_columns(col_index)
    for purify_round in range(ITERS):
        panel = lax.all_gather(to_pair(current, core), "row", axis=0, tiled=True)
        pieces = gather_cols(current)
        kept, given = call(
            square_body, where, live, pieces, panel, [], (rows_dev // CORE, CORE * BLK)
        )
        square = kept + send(given, TWIN)
        square_panel = gather_rows(square, "row")
        keep, give = call(
            step_body, where, live, pieces, square_panel, [kept, given], (rows_dev, BLK)
        )
        current = keep + send(give, TWIN)
    return current


def solution(mesh):
    return jax.shard_map(
        local,
        mesh=mesh,
        in_specs=(P("row", "col"), P()),
        out_specs=P("row", "col"),
        check_vma=False,
    )
```

```python
import jax
import jax.numpy as jnp
from jax import lax
from jax.experimental import pallas as pl
from jax.experimental.pallas import tpu as pltpu
from jax.sharding import PartitionSpec as P

BLK = 128
NNZ = 6
ITERS = 2
X_HI, Z, CORE = 2, 8, 2
Y, X_LO = 4, 2
GROUP = 4


def col_id(x_hi, z, core):
    return (x_hi * Z + z % Z) * CORE + core


COLS = [(x, z, c) for x in range(X_HI) for z in range(Z) for c in range(CORE)]
UP = [(col_id(x, z, c), col_id(x, z + 1, c)) for x, z, c in COLS]
DOWN = [(col_id(x, z, c), col_id(x, z - 1, c)) for x, z, c in COLS]
ACROSS = [(col_id(x, z, c), col_id(1 - x, z, c)) for x, z, c in COLS]
TWIN = [(col_id(x, z, c), col_id(x, z, 1 - c)) for x, z, c in COLS]
ROWS = [(y, x) for y in range(Y) for x in range(X_LO)]
NORTH = [(y * X_LO + x, (y + 1) % Y * X_LO + x) for y, x in ROWS]
SOUTH = [(y * X_LO + x, (y - 1) % Y * X_LO + x) for y, x in ROWS]
BESIDE = [(y * X_LO + x, y * X_LO + 1 - x) for y, x in ROWS]


def send(v, pairs):
    return lax.ppermute(v, "col", pairs)


def gather_rows(tile):
    move = lambda v, pairs: lax.ppermute(v, "row", pairs)
    beside = move(tile, BESIDE)
    south, north = move(tile, NORTH), move(tile, SOUTH)
    south_beside, north_beside = move(south, BESIDE), move(north, BESIDE)
    return [
        tile, beside, south, north, south_beside, north_beside,
        move(south, NORTH), move(north_beside, SOUTH),
    ]


def row_places(row):
    y, x_lo = row // X_LO, row % X_LO
    away = jnp.array([0, 0, -1, 1, -1, 1, 2, 2], jnp.int32)
    beside = jnp.array([0, 1, 0, 0, 1, 1, 0, 1], jnp.int32)
    return (y + away + Y) % Y * X_LO + (x_lo + beside) % X_LO


def gather_cols(tile):
    other = send(tile, ACROSS)
    pieces = [tile, other]
    up, down, other_up, other_down = tile, tile, other, other
    for _ in range(3):
        up, down = send(up, UP), send(down, DOWN)
        other_up, other_down = send(other_up, UP), send(other_down, DOWN)
        pieces += [up, down, other_up, other_down]
    return pieces + [send(up, UP), send(other_down, DOWN)]


def col_places(col):
    x_hi, z = col // (Z * CORE), (col // CORE) % Z
    away = jnp.array([0, 0, -1, 1, -1, 1, -2, 2, -2, 2, -3, 3, -3, 3, 4, 4], jnp.int32)
    across = jnp.array([0, 1, 0, 0, 1, 1, 0, 0, 1, 1, 0, 0, 1, 1, 0, 1], jnp.int32)
    return (x_hi + across) % X_HI * Z + (z + away + Z) % Z


def to_pair(tile, core):
    rows = tile.reshape(-1, CORE, BLK, BLK)
    mine = jnp.where(core == 0, rows[:, 0], rows[:, 1])
    other = send(jnp.where(core == 0, rows[:, 1], rows[:, 0]), TWIN)
    left = jnp.where(core == 0, mine, other)
    right = jnp.where(core == 0, other, mine)
    return jnp.concatenate([left, right], axis=2).reshape(-1, CORE * BLK)


def split(x):
    high = x.astype(jnp.bfloat16)
    return high, (x - high.astype(jnp.float32)).astype(jnp.bfloat16)


def partial_product(where, lefts, rights, high, low, total):
    rows = rights[0].shape[0]
    for j, piece in enumerate(rights):
        to = pl.ds(pl.multiple_of(where[len(lefts) + j] * rows, BLK), rows)
        high[to, :], low[to, :] = split(piece[...])
    dot = lambda a, b: jnp.dot(a, b, preferred_element_type=jnp.float32)
    for g in range(0, len(lefts), GROUP):
        slots = range(g, g + GROUP)
        left_high, left_low = split(jnp.concatenate([lefts[s][...] for s in slots], axis=1))
        at = [pl.ds(pl.multiple_of(where[s] * BLK, BLK), BLK) for s in slots]
        right_high = jnp.concatenate([high[i, :] for i in at], axis=0)
        right_low = jnp.concatenate([low[i, :] for i in at], axis=0)
        term = (dot(left_high, right_low) + dot(left_low, right_high)) + dot(left_high, right_high)
        total[...] = term if g == 0 else total[...] + term


def mask_pair(block, live, i):
    return jnp.concatenate(
        [live[CORE * i + c] * block[:, c * BLK : (c + 1) * BLK] for c in range(CORE)], axis=1
    )


def square_body(lefts, rights, where, live, *refs):
    left, right = refs[:lefts], refs[lefts : lefts + rights]
    keep, give, *scratch = refs[lefts + rights :]
    partial_product(where, left, right, *scratch)
    total = scratch[-1]
    core = where[lefts + rights]
    for q in range(keep.shape[0] // BLK):
        for out, i in ((keep, CORE * q + core), (give, CORE * q + 1 - core)):
            block = total[pl.ds(pl.multiple_of(i * BLK, BLK), BLK), :]
            out[pl.ds(q * BLK, BLK), :] = mask_pair(block, live, i)


def step_body(lefts, rights, where, live, *refs):
    left, right = refs[:lefts], refs[lefts : lefts + rights]
    kept, given, keep, give, *scratch = refs[lefts + rights :]
    partial_product(where, left, right, *scratch)
    total = scratch[-1]
    core = where[lefts + rights]
    first = core == 0
    for i in range(keep.shape[0] // BLK):
        rows = pl.ds(i * BLK, BLK)
        q = pl.ds(i // CORE * BLK, BLK)
        square = jnp.where(core == i % CORE, kept[q, :], given[q, :])
        part = 3.0 * square - 2.0 * mask_pair(total[rows, :], live, i)
        keep[rows, :] = jnp.where(first, part[:, :BLK], part[:, BLK:])
        give[rows, :] = jnp.where(first, part[:, BLK:], part[:, :BLK])


def call(body, where, live, left, right, extra, shape):
    rows, width = left[0].shape[0], right[0].shape[1]
    depth = len(left) * BLK
    vmem = pl.BlockSpec(memory_space=pltpu.VMEM)
    out = jax.ShapeDtypeStruct(shape, jnp.float32)
    return pl.pallas_call(
        lambda *refs: body(len(left), len(right), *refs),
        out_shape=(out, out),
        in_specs=[pl.BlockSpec(memory_space=pltpu.SMEM)] * 2
        + [vmem] * (len(left) + len(right) + len(extra)),
        out_specs=(vmem, vmem),
        scratch_shapes=[
            pltpu.VMEM((depth, width), jnp.bfloat16),
            pltpu.VMEM((depth, width), jnp.bfloat16),
            pltpu.VMEM((rows, width), jnp.float32),
        ],
        compiler_params=pltpu.CompilerParams(vmem_limit_bytes=16 << 20),
        cost_estimate=pl.CostEstimate(
            flops=6 * rows * depth * width,
            bytes_accessed=4 * (depth * (rows + width) + 2 * rows * width),
            transcendentals=0,
        ),
    )(where, live, *left, *right, *extra)


def local(density, pattern):
    rows_dev, cols_dev = density.shape
    row_number = lax.axis_index("row")
    col_index = lax.axis_index("col")
    core = col_index % CORE
    block_count = cols_dev * lax.axis_size("col") // BLK
    row_blocks = rows_dev // BLK
    listed = jnp.any(
        pattern[:, :, None] == jnp.arange(block_count, dtype=jnp.int32)[None, None, :], axis=1
    ).astype(jnp.float32)
    block_live = jnp.maximum(listed, listed.T)
    my_rows = lax.dynamic_slice_in_dim(block_live, row_number * row_blocks, row_blocks, 0)
    chip = lax.dynamic_slice_in_dim(my_rows, col_index - core, CORE, 1)
    tile_live = jnp.where(core == 0, chip[:, 0], chip[:, 1])
    tile_mask = jnp.repeat(tile_live, BLK)[:, None]
    live = chip.reshape(-1)
    global_rows = row_number * rows_dev + jnp.arange(rows_dev, dtype=jnp.int32)
    global_cols = col_index * cols_dev + jnp.arange(cols_dev, dtype=jnp.int32)
    identity = (global_rows[:, None] == global_cols[None, :]).astype(jnp.float32)
    current = 0.5 * identity + 0.45 / jnp.sqrt(jnp.float32(2 * NNZ * BLK)) * tile_mask * density
    where = jnp.concatenate(
        [col_places(col_index), row_places(row_number), core[None]]
    ).astype(jnp.int32)
    for purify_round in range(ITERS):
        left = gather_cols(current)
        right = gather_rows(to_pair(current, core))
        kept, given = call(
            square_body, where, live, left, right, [], (rows_dev // CORE, CORE * BLK)
        )
        square = gather_rows(kept + send(given, TWIN))
        keep, give = call(
            step_body, where, live, left, square, [kept, given], (rows_dev, BLK)
        )
        current = keep + send(give, TWIN)
    return current


def solution(mesh):
    return jax.shard_map(
        local,
        mesh=mesh,
        in_specs=(P("row", "col"), P()),
        out_specs=P("row", "col"),
        check_vma=False,
    )
```

```python
import jax
import jax.numpy as jnp
from jax import lax
from jax.experimental import pallas as pl
from jax.experimental.pallas import tpu as pltpu
from jax.sharding import PartitionSpec as P

BLK = 128
NNZ = 6
ITERS = 2
X_HI, Z, CORE = 2, 8, 2
Y, X_LO = 4, 2
GROUP = 4


def col_id(x_hi, z, core):
    return (x_hi * Z + z % Z) * CORE + core


COLS = [(x, z, c) for x in range(X_HI) for z in range(Z) for c in range(CORE)]
UP = [(col_id(x, z, c), col_id(x, z + 1, c)) for x, z, c in COLS]
DOWN = [(col_id(x, z, c), col_id(x, z - 1, c)) for x, z, c in COLS]
ACROSS = [(col_id(x, z, c), col_id(1 - x, z, c)) for x, z, c in COLS]
TWIN = [(col_id(x, z, c), col_id(x, z, 1 - c)) for x, z, c in COLS]
ROWS = [(y, x) for y in range(Y) for x in range(X_LO)]
NORTH = [(y * X_LO + x, (y + 1) % Y * X_LO + x) for y, x in ROWS]
SOUTH = [(y * X_LO + x, (y - 1) % Y * X_LO + x) for y, x in ROWS]
OPPOSITE = [(y * X_LO + x, (y + 2) % Y * X_LO + x) for y, x in ROWS]
BESIDE = [(y * X_LO + x, y * X_LO + 1 - x) for y, x in ROWS]


def send(v, pairs):
    return lax.ppermute(v, "col", pairs)


def gather_rows(tile):
    move = lambda v, pairs: lax.ppermute(v, "row", pairs)
    first = move(tile, BESIDE), move(tile, NORTH), move(tile, SOUTH)
    beside, south, north = lax.optimization_barrier(first)
    return [
        tile, beside, south, north,
        move(south, BESIDE), move(north, BESIDE), move(south, NORTH), move(beside, OPPOSITE),
    ]


def row_places(row):
    y, x_lo = row // X_LO, row % X_LO
    away = jnp.array([0, 0, -1, 1, -1, 1, 2, 2], jnp.int32)
    beside = jnp.array([0, 1, 0, 0, 1, 1, 0, 1], jnp.int32)
    return (y + away + Y) % Y * X_LO + (x_lo + beside) % X_LO


def gather_cols(tile):
    other = send(tile, ACROSS)
    pieces = [tile, other]
    up, down, other_up, other_down = tile, tile, other, other
    for _ in range(3):
        up, down = send(up, UP), send(down, DOWN)
        other_up, other_down = send(other_up, UP), send(other_down, DOWN)
        pieces += [up, down, other_up, other_down]
    return pieces + [send(up, UP), send(other_down, DOWN)]


def col_places(col):
    x_hi, z = col // (Z * CORE), (col // CORE) % Z
    away = jnp.array([0, 0, -1, 1, -1, 1, -2, 2, -2, 2, -3, 3, -3, 3, 4, 4], jnp.int32)
    across = jnp.array([0, 1, 0, 0, 1, 1, 0, 0, 1, 1, 0, 0, 1, 1, 0, 1], jnp.int32)
    return (x_hi + across) % X_HI * Z + (z + away + Z) % Z


def to_pair(tile, core):
    rows = tile.reshape(-1, CORE, BLK, BLK)
    mine = jnp.where(core == 0, rows[:, 0], rows[:, 1])
    other = send(jnp.where(core == 0, rows[:, 1], rows[:, 0]), TWIN)
    left = jnp.where(core == 0, mine, other)
    right = jnp.where(core == 0, other, mine)
    return jnp.concatenate([left, right], axis=2).reshape(-1, CORE * BLK)


def split(x):
    high = x.astype(jnp.bfloat16)
    return high, (x - high.astype(jnp.float32)).astype(jnp.bfloat16)


def partial_product(where, lefts, rights, high, low, total):
    rows = rights[0].shape[0]
    for j, piece in enumerate(rights):
        to = pl.ds(pl.multiple_of(where[len(lefts) + j] * rows, BLK), rows)
        high[to, :], low[to, :] = split(piece[...])
    dot = lambda a, b: jnp.dot(a, b, preferred_element_type=jnp.float32)
    for g in range(0, len(lefts), GROUP):
        slots = range(g, g + GROUP)
        left_high, left_low = split(jnp.concatenate([lefts[s][...] for s in slots], axis=1))
        at = [pl.ds(pl.multiple_of(where[s] * BLK, BLK), BLK) for s in slots]
        right_high = jnp.concatenate([high[i, :] for i in at], axis=0)
        right_low = jnp.concatenate([low[i, :] for i in at], axis=0)
        term = (dot(left_high, right_low) + dot(left_low, right_high)) + dot(left_high, right_high)
        total[...] = term if g == 0 else total[...] + term


def mask_pair(block, live, i):
    return jnp.concatenate(
        [live[CORE * i + c] * block[:, c * BLK : (c + 1) * BLK] for c in range(CORE)], axis=1
    )


def square_body(lefts, rights, where, live, *refs):
    left, right = refs[:lefts], refs[lefts : lefts + rights]
    keep, give, *scratch = refs[lefts + rights :]
    partial_product(where, left, right, *scratch)
    total = scratch[-1]
    core = where[lefts + rights]
    for q in range(keep.shape[0] // BLK):
        for out, i in ((keep, CORE * q + core), (give, CORE * q + 1 - core)):
            block = total[pl.ds(pl.multiple_of(i * BLK, BLK), BLK), :]
            out[pl.ds(q * BLK, BLK), :] = mask_pair(block, live, i)


def step_body(lefts, rights, where, live, *refs):
    left, right = refs[:lefts], refs[lefts : lefts + rights]
    kept, given, keep, give, *scratch = refs[lefts + rights :]
    partial_product(where, left, right, *scratch)
    total = scratch[-1]
    core = where[lefts + rights]
    first = core == 0
    for i in range(keep.shape[0] // BLK):
        rows = pl.ds(i * BLK, BLK)
        q = pl.ds(i // CORE * BLK, BLK)
        square = jnp.where(core == i % CORE, kept[q, :], given[q, :])
        part = 3.0 * square - 2.0 * mask_pair(total[rows, :], live, i)
        keep[rows, :] = jnp.where(first, part[:, :BLK], part[:, BLK:])
        give[rows, :] = jnp.where(first, part[:, BLK:], part[:, :BLK])


def call(body, where, live, left, right, extra, shape):
    rows, width = left[0].shape[0], right[0].shape[1]
    depth = len(left) * BLK
    vmem = pl.BlockSpec(memory_space=pltpu.VMEM)
    out = jax.ShapeDtypeStruct(shape, jnp.float32)
    return pl.pallas_call(
        lambda *refs: body(len(left), len(right), *refs),
        out_shape=(out, out),
        in_specs=[pl.BlockSpec(memory_space=pltpu.SMEM)] * 2
        + [vmem] * (len(left) + len(right) + len(extra)),
        out_specs=(vmem, vmem),
        scratch_shapes=[
            pltpu.VMEM((depth, width), jnp.bfloat16),
            pltpu.VMEM((depth, width), jnp.bfloat16),
            pltpu.VMEM((rows, width), jnp.float32),
        ],
        compiler_params=pltpu.CompilerParams(vmem_limit_bytes=16 << 20),
        cost_estimate=pl.CostEstimate(
            flops=6 * rows * depth * width,
            bytes_accessed=4 * (depth * (rows + width) + 2 * rows * width),
            transcendentals=0,
        ),
    )(where, live, *left, *right, *extra)


def local(density, pattern):
    rows_dev, cols_dev = density.shape
    row_number = lax.axis_index("row")
    col_index = lax.axis_index("col")
    core = col_index % CORE
    block_count = cols_dev * lax.axis_size("col") // BLK
    row_blocks = rows_dev // BLK
    listed = jnp.any(
        pattern[:, :, None] == jnp.arange(block_count, dtype=jnp.int32)[None, None, :], axis=1
    ).astype(jnp.float32)
    block_live = jnp.maximum(listed, listed.T)
    my_rows = lax.dynamic_slice_in_dim(block_live, row_number * row_blocks, row_blocks, 0)
    chip = lax.dynamic_slice_in_dim(my_rows, col_index - core, CORE, 1)
    tile_live = jnp.where(core == 0, chip[:, 0], chip[:, 1])
    tile_mask = jnp.repeat(tile_live, BLK)[:, None]
    live = chip.reshape(-1)
    global_rows = row_number * rows_dev + jnp.arange(rows_dev, dtype=jnp.int32)
    global_cols = col_index * cols_dev + jnp.arange(cols_dev, dtype=jnp.int32)
    identity = (global_rows[:, None] == global_cols[None, :]).astype(jnp.float32)
    current = 0.5 * identity + 0.45 / jnp.sqrt(jnp.float32(2 * NNZ * BLK)) * tile_mask * density
    where = jnp.concatenate(
        [col_places(col_index), row_places(row_number), core[None]]
    ).astype(jnp.int32)
    def purify(_, current):
        left = gather_cols(current)
        right = gather_rows(to_pair(current, core))
        kept, given = call(
            square_body, where, live, left, right, [], (rows_dev // CORE, CORE * BLK)
        )
        square = gather_rows(kept + send(given, TWIN))
        keep, give = call(
            step_body, where, live, left, square, [kept, given], (rows_dev, BLK)
        )
        return keep + send(give, TWIN)

    return lax.fori_loop(0, ITERS, purify, current)


def solution(mesh):
    return jax.shard_map(
        local,
        mesh=mesh,
        in_specs=(P("row", "col"), P()),
        out_specs=P("row", "col"),
        check_vma=False,
    )
```

```python
import jax
import jax.numpy as jnp
from jax import lax
from jax.experimental import pallas as pl
from jax.experimental.pallas import tpu as pltpu
from jax.sharding import PartitionSpec as P

BLK = 128
NNZ = 6
ITERS = 2
X_HI, Z, CORE = 2, 8, 2
Y, X_LO = 4, 2
GROUP = 4


def col_id(x_hi, z, core):
    return (x_hi * Z + z % Z) * CORE + core


COLS = [(x, z, c) for x in range(X_HI) for z in range(Z) for c in range(CORE)]
UP = [(col_id(x, z, c), col_id(x, z + 1, c)) for x, z, c in COLS]
DOWN = [(col_id(x, z, c), col_id(x, z - 1, c)) for x, z, c in COLS]
ACROSS = [(col_id(x, z, c), col_id(1 - x, z, c)) for x, z, c in COLS]
TWIN = [(col_id(x, z, c), col_id(x, z, 1 - c)) for x, z, c in COLS]
ROWS = [(y, x) for y in range(Y) for x in range(X_LO)]
NORTH = [(y * X_LO + x, (y + 1) % Y * X_LO + x) for y, x in ROWS]
SOUTH = [(y * X_LO + x, (y - 1) % Y * X_LO + x) for y, x in ROWS]
OPPOSITE = [(y * X_LO + x, (y + 2) % Y * X_LO + x) for y, x in ROWS]
BESIDE = [(y * X_LO + x, y * X_LO + 1 - x) for y, x in ROWS]


def send(v, pairs):
    return lax.ppermute(v, "col", pairs)


def gather_rows(tile):
    move = lambda v, pairs: lax.ppermute(v, "row", pairs)
    first = move(tile, BESIDE), move(tile, NORTH), move(tile, SOUTH)
    beside, south, north = lax.optimization_barrier(first)
    return [
        tile, beside, south, north,
        move(south, BESIDE), move(north, BESIDE), move(south, NORTH), move(beside, OPPOSITE),
    ]


def row_places(row):
    y, x_lo = row // X_LO, row % X_LO
    s = jnp.arange(Y * X_LO, dtype=jnp.int32)
    away = jnp.where(s < 2, 0, jnp.where(s > 5, 2, 2 * (s % 2) - 1))
    beside = jnp.where(s < 2, s, jnp.where(s > 5, s % 2, s // 4))
    return ((y + away + Y) % Y * X_LO + (x_lo + beside) % X_LO) * CORE


def gather_cols(tile):
    other = send(tile, ACROSS)
    pieces = [tile, other]
    up, down, other_up, other_down = tile, tile, other, other
    for _ in range(3):
        up, down = send(up, UP), send(down, DOWN)
        other_up, other_down = send(other_up, UP), send(other_down, DOWN)
        pieces += [up, down, other_up, other_down]
    return pieces + [send(up, UP), send(other_down, DOWN)]


def col_places(col):
    x_hi, z = col // (Z * CORE), (col // CORE) % Z
    s = jnp.arange(X_HI * Z, dtype=jnp.int32)
    hop = (s + 2) // 4
    away = jnp.where(s % 2 == 0, -hop, hop)
    across = jnp.where(hop == 0, s, jnp.where(hop == 4, s - 14, (s + 2) // 2))
    return (x_hi + across) % X_HI * Z + (z + away + Z) % Z


def to_pair(tile, core):
    rows = tile.reshape(-1, CORE, BLK, BLK)
    mine = jnp.where(core == 0, rows[:, 0], rows[:, 1])
    other = send(jnp.where(core == 0, rows[:, 1], rows[:, 0]), TWIN)
    left = jnp.where(core == 0, mine, other)
    right = jnp.where(core == 0, other, mine)
    return jnp.concatenate([left, right], axis=2).reshape(-1, CORE * BLK)


def split(x):
    high = x.astype(jnp.bfloat16)
    return high, (x - high.astype(jnp.float32)).astype(jnp.bfloat16)


def partial_product(where, lefts, rights, high, low, total):
    for j, piece in enumerate(rights):
        to = pl.ds(pl.multiple_of(where[len(lefts) + j] * BLK, BLK), piece.shape[0])
        high[to, :], low[to, :] = split(piece[...])
    dot = lambda a, b: jnp.dot(a, b, preferred_element_type=jnp.float32)
    for g in range(0, len(lefts), GROUP):
        slots = range(g, g + GROUP)
        left_high, left_low = split(jnp.concatenate([lefts[s][...] for s in slots], axis=1))
        at = [pl.ds(pl.multiple_of(where[s] * BLK, BLK), BLK) for s in slots]
        right_high = jnp.concatenate([high[i, :] for i in at], axis=0)
        right_low = jnp.concatenate([low[i, :] for i in at], axis=0)
        term = (dot(left_high, right_low) + dot(left_low, right_high)) + dot(left_high, right_high)
        total[...] = term if g == 0 else total[...] + term


def mask_pair(block, live, i):
    return jnp.concatenate(
        [live[CORE * i + c] * block[:, c * BLK : (c + 1) * BLK] for c in range(CORE)], axis=1
    )


def square_body(lefts, rights, where, live, *refs):
    left, right = refs[:lefts], refs[lefts : lefts + rights]
    keep, give, *scratch = refs[lefts + rights :]
    partial_product(where, left, right, *scratch)
    total = scratch[-1]
    core = where[lefts + rights]
    for q in range(keep.shape[0] // BLK):
        for out, i in ((keep, CORE * q + core), (give, CORE * q + 1 - core)):
            block = total[pl.ds(pl.multiple_of(i * BLK, BLK), BLK), :]
            out[pl.ds(q * BLK, BLK), :] = mask_pair(block, live, i)


def step_body(lefts, rights, where, live, *refs):
    left, right = refs[:lefts], refs[lefts : lefts + rights]
    kept, given, keep, give, *scratch = refs[lefts + rights :]
    partial_product(where, left, right, *scratch)
    total = scratch[-1]
    core = where[lefts + rights]
    first = core == 0
    for i in range(keep.shape[0] // BLK):
        rows = pl.ds(i * BLK, BLK)
        q = pl.ds(i // CORE * BLK, BLK)
        square = jnp.where(core == i % CORE, kept[q, :], given[q, :])
        part = 3.0 * square - 2.0 * mask_pair(total[rows, :], live, i)
        keep[rows, :] = jnp.where(first, part[:, :BLK], part[:, BLK:])
        give[rows, :] = jnp.where(first, part[:, BLK:], part[:, :BLK])


def call(body, where, live, left, right, extra, shape):
    rows, width = left[0].shape[0], right[0].shape[1]
    depth = len(left) * BLK
    vmem = pl.BlockSpec(memory_space=pltpu.VMEM)
    out = jax.ShapeDtypeStruct(shape, jnp.float32)
    return pl.pallas_call(
        lambda *refs: body(len(left), len(right), *refs),
        out_shape=(out, out),
        in_specs=[pl.BlockSpec(memory_space=pltpu.SMEM)] * 2
        + [vmem] * (len(left) + len(right) + len(extra)),
        out_specs=(vmem, vmem),
        scratch_shapes=[
            pltpu.VMEM((depth, width), jnp.bfloat16),
            pltpu.VMEM((depth, width), jnp.bfloat16),
            pltpu.VMEM((rows, width), jnp.float32),
        ],
        compiler_params=pltpu.CompilerParams(vmem_limit_bytes=16 << 20),
        cost_estimate=pl.CostEstimate(
            flops=6 * rows * depth * width,
            bytes_accessed=4 * (depth * (rows + width) + 2 * rows * width),
            transcendentals=0,
        ),
    )(where, live, *left, *right, *extra)


def local(density, pattern):
    rows_dev, cols_dev = density.shape
    row_number = lax.axis_index("row")
    col_index = lax.axis_index("col")
    core = col_index % CORE
    block_count = cols_dev * lax.axis_size("col") // BLK
    row_blocks = rows_dev // BLK
    listed = jnp.any(
        pattern[:, :, None] == jnp.arange(block_count, dtype=jnp.int32)[None, None, :], axis=1
    ).astype(jnp.float32)
    block_live = jnp.maximum(listed, listed.T)
    my_rows = lax.dynamic_slice_in_dim(block_live, row_number * row_blocks, row_blocks, 0)
    chip = lax.dynamic_slice_in_dim(my_rows, col_index - core, CORE, 1)
    tile_live = jnp.where(core == 0, chip[:, 0], chip[:, 1])
    tile_mask = jnp.repeat(tile_live, BLK)[:, None]
    live = chip.reshape(-1)
    global_rows = row_number * rows_dev + jnp.arange(rows_dev, dtype=jnp.int32)
    global_cols = col_index * cols_dev + jnp.arange(cols_dev, dtype=jnp.int32)
    identity = (global_rows[:, None] == global_cols[None, :]).astype(jnp.float32)
    current = 0.5 * identity + 0.45 / jnp.sqrt(jnp.float32(2 * NNZ * BLK)) * tile_mask * density
    where = jnp.concatenate(
        [col_places(col_index), row_places(row_number), core[None]]
    ).astype(jnp.int32)

    def purify(_, current):
        left = gather_cols(current)
        pair, left[1] = lax.optimization_barrier((to_pair(current, core), left[1]))
        right = gather_rows(pair)
        kept, given = call(
            square_body, where, live, left, right, [], (rows_dev // CORE, CORE * BLK)
        )
        square = gather_rows(kept + send(given, TWIN))
        keep, give = call(
            step_body, where, live, left, square, [kept, given], (rows_dev, BLK)
        )
        return keep + send(give, TWIN)

    return lax.fori_loop(0, ITERS, purify, current)


def solution(mesh):
    return jax.shard_map(
        local,
        mesh=mesh,
        in_specs=(P("row", "col"), P()),
        out_specs=P("row", "col"),
        check_vma=False,
    )
```

```python
import jax
import jax.numpy as jnp
from jax import lax
from jax.experimental import pallas as pl
from jax.experimental.pallas import tpu as pltpu
from jax.sharding import PartitionSpec as P

BLK = 128
NNZ = 6
ITERS = 2
X_HI, Z, CORE = 2, 8, 2
Y, X_LO = 4, 2
GROUP = 4


def col_id(x_hi, z, core):
    return (x_hi * Z + z % Z) * CORE + core


COLS = [(x, z, c) for x in range(X_HI) for z in range(Z) for c in range(CORE)]
UP = [(col_id(x, z, c), col_id(x, z + 1, c)) for x, z, c in COLS]
DOWN = [(col_id(x, z, c), col_id(x, z - 1, c)) for x, z, c in COLS]
ACROSS = [(col_id(x, z, c), col_id(1 - x, z, c)) for x, z, c in COLS]
TWIN = [(col_id(x, z, c), col_id(x, z, 1 - c)) for x, z, c in COLS]
ROWS = [(y, x) for y in range(Y) for x in range(X_LO)]
NORTH = [(y * X_LO + x, (y + 1) % Y * X_LO + x) for y, x in ROWS]
SOUTH = [(y * X_LO + x, (y - 1) % Y * X_LO + x) for y, x in ROWS]
OPPOSITE = [(y * X_LO + x, (y + 2) % Y * X_LO + x) for y, x in ROWS]
BESIDE = [(y * X_LO + x, y * X_LO + 1 - x) for y, x in ROWS]


def send(v, pairs):
    return lax.ppermute(v, "col", pairs)


def gather_rows(tile):
    move = lambda v, pairs: lax.ppermute(v, "row", pairs)
    north = move(tile, SOUTH)
    beside, south = lax.optimization_barrier((move(tile, BESIDE), move(tile, NORTH)))
    return [
        tile, beside, south, north,
        move(south, BESIDE), move(north, BESIDE), move(south, NORTH), move(beside, OPPOSITE),
    ]


def row_places(row):
    y, x_lo = row // X_LO, row % X_LO
    s = jnp.arange(Y * X_LO, dtype=jnp.int32)
    away = jnp.where(s < 2, 0, jnp.where(s > 5, 2, 2 * (s % 2) - 1))
    beside = jnp.where(s < 2, s, jnp.where(s > 5, s % 2, s // 4))
    return ((y + away + Y) % Y * X_LO + (x_lo + beside) % X_LO) * CORE


def gather_cols(tile):
    other = send(tile, ACROSS)
    pieces = [tile, other]
    up, down, other_up, other_down = tile, tile, other, other
    for _ in range(3):
        up, down = send(up, UP), send(down, DOWN)
        other_up, other_down = send(other_up, UP), send(other_down, DOWN)
        pieces += [up, down, other_up, other_down]
    return pieces + [send(up, UP), send(other_down, DOWN)]


def col_places(col):
    x_hi, z = col // (Z * CORE), (col // CORE) % Z
    s = jnp.arange(X_HI * Z, dtype=jnp.int32)
    hop = (s + 2) // 4
    away = jnp.where(s % 2 == 0, -hop, hop)
    across = jnp.where(hop == 0, s, jnp.where(hop == 4, s - 14, (s + 2) // 2))
    return (x_hi + across) % X_HI * Z + (z + away + Z) % Z


def to_pair(tile, core):
    rows = tile.reshape(-1, CORE, BLK, BLK)
    mine = jnp.where(core == 0, rows[:, 0], rows[:, 1])
    other = send(jnp.where(core == 0, rows[:, 1], rows[:, 0]), TWIN)
    left = jnp.where(core == 0, mine, other)
    right = jnp.where(core == 0, other, mine)
    return jnp.concatenate([left, right], axis=2).reshape(-1, CORE * BLK)


def split(x):
    high = x.astype(jnp.bfloat16)
    return high, (x - high.astype(jnp.float32)).astype(jnp.bfloat16)


def partial_product(where, lefts, rights, high, low, total):
    for j, piece in enumerate(rights):
        to = pl.ds(pl.multiple_of(where[len(lefts) + j] * BLK, BLK), piece.shape[0])
        high[to, :], low[to, :] = split(piece[...])
    dot = lambda a, b: jnp.dot(a, b, preferred_element_type=jnp.float32)
    for g in range(0, len(lefts), GROUP):
        slots = range(g, g + GROUP)
        left_high, left_low = split(jnp.concatenate([lefts[s][...] for s in slots], axis=1))
        at = [pl.ds(pl.multiple_of(where[s] * BLK, BLK), BLK) for s in slots]
        right_high = jnp.concatenate([high[i, :] for i in at], axis=0)
        right_low = jnp.concatenate([low[i, :] for i in at], axis=0)
        term = (dot(left_high, right_low) + dot(left_low, right_high)) + dot(left_high, right_high)
        total[...] = term if g == 0 else total[...] + term


def mask_pair(block, live, i):
    return jnp.concatenate(
        [live[CORE * i + c] * block[:, c * BLK : (c + 1) * BLK] for c in range(CORE)], axis=1
    )


def square_body(lefts, rights, where, live, *refs):
    left, right = refs[:lefts], refs[lefts : lefts + rights]
    keep, give, *scratch = refs[lefts + rights :]
    partial_product(where, left, right, *scratch)
    total = scratch[-1]
    core = where[lefts + rights]
    for q in range(keep.shape[0] // BLK):
        for out, i in ((keep, CORE * q + core), (give, CORE * q + 1 - core)):
            block = total[pl.ds(pl.multiple_of(i * BLK, BLK), BLK), :]
            out[pl.ds(q * BLK, BLK), :] = mask_pair(block, live, i)


def step_body(lefts, rights, where, live, *refs):
    left, right = refs[:lefts], refs[lefts : lefts + rights]
    kept, given, keep, give, *scratch = refs[lefts + rights :]
    partial_product(where, left, right, *scratch)
    total = scratch[-1]
    core = where[lefts + rights]
    first = core == 0
    for i in range(keep.shape[0] // BLK):
        rows = pl.ds(i * BLK, BLK)
        q = pl.ds(i // CORE * BLK, BLK)
        square = jnp.where(core == i % CORE, kept[q, :], given[q, :])
        part = 3.0 * square - 2.0 * mask_pair(total[rows, :], live, i)
        keep[rows, :] = jnp.where(first, part[:, :BLK], part[:, BLK:])
        give[rows, :] = jnp.where(first, part[:, BLK:], part[:, :BLK])


def call(body, where, live, left, right, extra, shape):
    rows, width = left[0].shape[0], right[0].shape[1]
    depth = len(left) * BLK
    vmem = pl.BlockSpec(memory_space=pltpu.VMEM)
    out = jax.ShapeDtypeStruct(shape, jnp.float32)
    return pl.pallas_call(
        lambda *refs: body(len(left), len(right), *refs),
        out_shape=(out, out),
        in_specs=[pl.BlockSpec(memory_space=pltpu.SMEM)] * 2
        + [vmem] * (len(left) + len(right) + len(extra)),
        out_specs=(vmem, vmem),
        scratch_shapes=[
            pltpu.VMEM((depth, width), jnp.bfloat16),
            pltpu.VMEM((depth, width), jnp.bfloat16),
            pltpu.VMEM((rows, width), jnp.float32),
        ],
        compiler_params=pltpu.CompilerParams(vmem_limit_bytes=16 << 20),
        cost_estimate=pl.CostEstimate(
            flops=6 * rows * depth * width,
            bytes_accessed=4 * (depth * (rows + width) + 2 * rows * width),
            transcendentals=0,
        ),
    )(where, live, *left, *right, *extra)


def local(density, pattern):
    rows_dev, cols_dev = density.shape
    row_number = lax.axis_index("row")
    col_index = lax.axis_index("col")
    core = col_index % CORE
    block_count = cols_dev * lax.axis_size("col") // BLK
    row_blocks = rows_dev // BLK
    listed = jnp.any(
        pattern[:, :, None] == jnp.arange(block_count, dtype=jnp.int32)[None, None, :], axis=1
    ).astype(jnp.float32)
    block_live = jnp.maximum(listed, listed.T)
    my_rows = lax.dynamic_slice_in_dim(block_live, row_number * row_blocks, row_blocks, 0)
    chip = lax.dynamic_slice_in_dim(my_rows, col_index - core, CORE, 1)
    tile_live = jnp.where(core == 0, chip[:, 0], chip[:, 1])
    tile_mask = jnp.repeat(tile_live, BLK)[:, None]
    live = chip.reshape(-1)
    global_rows = row_number * rows_dev + jnp.arange(rows_dev, dtype=jnp.int32)
    global_cols = col_index * cols_dev + jnp.arange(cols_dev, dtype=jnp.int32)
    identity = (global_rows[:, None] == global_cols[None, :]).astype(jnp.float32)
    current = 0.5 * identity + 0.45 / jnp.sqrt(jnp.float32(2 * NNZ * BLK)) * tile_mask * density
    where = jnp.concatenate(
        [col_places(col_index), row_places(row_number), core[None]]
    ).astype(jnp.int32)

    def purify(_, current):
        left = gather_cols(current)
        pair, left[1] = lax.optimization_barrier((to_pair(current, core), left[1]))
        right = gather_rows(pair)
        kept, given = call(
            square_body, where, live, left, right, [], (rows_dev // CORE, CORE * BLK)
        )
        square = gather_rows(kept + send(given, TWIN))
        keep, give = call(
            step_body, where, live, left, square, [kept, given], (rows_dev, BLK)
        )
        return keep + send(give, TWIN)

    return lax.fori_loop(0, ITERS, purify, current)


def solution(mesh):
    return jax.shard_map(
        local,
        mesh=mesh,
        in_specs=(P("row", "col"), P()),
        out_specs=P("row", "col"),
        check_vma=False,
    )
```

```python
import jax
import jax.numpy as jnp
from jax import lax
from jax.experimental import pallas as pl
from jax.experimental.pallas import tpu as pltpu
from jax.sharding import PartitionSpec as P

BLK = 128
NNZ = 6
ITERS = 2
X_HI, Z, CORE = 2, 8, 2
Y, X_LO = 4, 2
GROUP = 4


def col_id(x_hi, z, core):
    return (x_hi * Z + z % Z) * CORE + core


COLS = [(x, z, c) for x in range(X_HI) for z in range(Z) for c in range(CORE)]
UP = [(col_id(x, z, c), col_id(x, z + 1, c)) for x, z, c in COLS]
DOWN = [(col_id(x, z, c), col_id(x, z - 1, c)) for x, z, c in COLS]
ACROSS = [(col_id(x, z, c), col_id(1 - x, z, c)) for x, z, c in COLS]
TWIN = [(col_id(x, z, c), col_id(x, z, 1 - c)) for x, z, c in COLS]
ROWS = [(y, x) for y in range(Y) for x in range(X_LO)]
NORTH = [(y * X_LO + x, (y + 1) % Y * X_LO + x) for y, x in ROWS]
SOUTH = [(y * X_LO + x, (y - 1) % Y * X_LO + x) for y, x in ROWS]
OPPOSITE = [(y * X_LO + x, (y + 2) % Y * X_LO + x) for y, x in ROWS]
BESIDE = [(y * X_LO + x, y * X_LO + 1 - x) for y, x in ROWS]


def send(v, pairs):
    return lax.ppermute(v, "col", pairs)


def gather_rows(tile):
    move = lambda v, pairs: lax.ppermute(v, "row", pairs)
    north = move(tile, SOUTH)
    next_to = move(tile, BESIDE)
    opposite = move(next_to, OPPOSITE)
    beside, south = lax.optimization_barrier((next_to, move(tile, NORTH)))
    return [
        tile, beside, south, north,
        move(south, BESIDE), move(north, BESIDE), move(south, NORTH), opposite,
    ]


def row_places(row):
    y, x_lo = row // X_LO, row % X_LO
    s = jnp.arange(Y * X_LO, dtype=jnp.int32)
    away = jnp.where(s < 2, 0, jnp.where(s > 5, 2, 2 * (s % 2) - 1))
    beside = jnp.where(s < 2, s, jnp.where(s > 5, s % 2, s // 4))
    return ((y + away + Y) % Y * X_LO + (x_lo + beside) % X_LO) * CORE


def gather_cols(tile):
    other = send(tile, ACROSS)
    pieces = [tile, other]
    up, down, other_up, other_down = tile, tile, other, other
    for _ in range(3):
        up, down = send(up, UP), send(down, DOWN)
        other_up, other_down = send(other_up, UP), send(other_down, DOWN)
        pieces += [up, down, other_up, other_down]
    return pieces + [send(up, UP), send(other_down, DOWN)]


def col_places(col):
    x_hi, z = col // (Z * CORE), (col // CORE) % Z
    s = jnp.arange(X_HI * Z, dtype=jnp.int32)
    hop = (s + 2) // 4
    away = jnp.where(s % 2 == 0, -hop, hop)
    across = jnp.where(hop == 0, s, jnp.where(hop == 4, s - 14, (s + 2) // 2))
    return (x_hi + across) % X_HI * Z + (z + away + Z) % Z


def to_pair(tile, core):
    rows = tile.reshape(-1, CORE, BLK, BLK)
    mine = jnp.where(core == 0, rows[:, 0], rows[:, 1])
    other = send(jnp.where(core == 0, rows[:, 1], rows[:, 0]), TWIN)
    left = jnp.where(core == 0, mine, other)
    right = jnp.where(core == 0, other, mine)
    return jnp.concatenate([left, right], axis=2).reshape(-1, CORE * BLK)


def split(x):
    high = x.astype(jnp.bfloat16)
    return high, (x - high.astype(jnp.float32)).astype(jnp.bfloat16)


def partial_product(where, lefts, rights, high, low, total):
    for j, piece in enumerate(rights):
        to = pl.ds(pl.multiple_of(where[len(lefts) + j] * BLK, BLK), piece.shape[0])
        high[to, :], low[to, :] = split(piece[...])
    dot = lambda a, b: jnp.dot(a, b, preferred_element_type=jnp.float32)
    for g in range(0, len(lefts), GROUP):
        slots = range(g, g + GROUP)
        left_high, left_low = split(jnp.concatenate([lefts[s][...] for s in slots], axis=1))
        at = [pl.ds(pl.multiple_of(where[s] * BLK, BLK), BLK) for s in slots]
        right_high = jnp.concatenate([high[i, :] for i in at], axis=0)
        right_low = jnp.concatenate([low[i, :] for i in at], axis=0)
        term = (dot(left_high, right_low) + dot(left_low, right_high)) + dot(left_high, right_high)
        total[...] = term if g == 0 else total[...] + term


def mask_pair(block, live, i):
    return jnp.concatenate(
        [live[CORE * i + c] * block[:, c * BLK : (c + 1) * BLK] for c in range(CORE)], axis=1
    )


def square_body(lefts, rights, where, live, *refs):
    left, right = refs[:lefts], refs[lefts : lefts + rights]
    keep, give, *scratch = refs[lefts + rights :]
    partial_product(where, left, right, *scratch)
    total = scratch[-1]
    core = where[lefts + rights]
    for q in range(keep.shape[0] // BLK):
        for out, i in ((keep, CORE * q + core), (give, CORE * q + 1 - core)):
            block = total[pl.ds(pl.multiple_of(i * BLK, BLK), BLK), :]
            out[pl.ds(q * BLK, BLK), :] = mask_pair(block, live, i)


def step_body(lefts, rights, where, live, *refs):
    left, right = refs[:lefts], refs[lefts : lefts + rights]
    kept, given, keep, give, *scratch = refs[lefts + rights :]
    partial_product(where, left, right, *scratch)
    total = scratch[-1]
    core = where[lefts + rights]
    first = core == 0
    for i in range(keep.shape[0] // BLK):
        rows = pl.ds(i * BLK, BLK)
        q = pl.ds(i // CORE * BLK, BLK)
        square = jnp.where(core == i % CORE, kept[q, :], given[q, :])
        part = 3.0 * square - 2.0 * mask_pair(total[rows, :], live, i)
        keep[rows, :] = jnp.where(first, part[:, :BLK], part[:, BLK:])
        give[rows, :] = jnp.where(first, part[:, BLK:], part[:, :BLK])


def call(body, where, live, left, right, extra, shape):
    rows, width = left[0].shape[0], right[0].shape[1]
    depth = len(left) * BLK
    vmem = pl.BlockSpec(memory_space=pltpu.VMEM)
    out = jax.ShapeDtypeStruct(shape, jnp.float32)
    return pl.pallas_call(
        lambda *refs: body(len(left), len(right), *refs),
        out_shape=(out, out),
        in_specs=[pl.BlockSpec(memory_space=pltpu.SMEM)] * 2
        + [vmem] * (len(left) + len(right) + len(extra)),
        out_specs=(vmem, vmem),
        scratch_shapes=[
            pltpu.VMEM((depth, width), jnp.bfloat16),
            pltpu.VMEM((depth, width), jnp.bfloat16),
            pltpu.VMEM((rows, width), jnp.float32),
        ],
        compiler_params=pltpu.CompilerParams(vmem_limit_bytes=16 << 20),
        cost_estimate=pl.CostEstimate(
            flops=6 * rows * depth * width,
            bytes_accessed=4 * (depth * (rows + width) + 2 * rows * width),
            transcendentals=0,
        ),
    )(where, live, *left, *right, *extra)


def local(density, pattern):
    rows_dev, cols_dev = density.shape
    row_number = lax.axis_index("row")
    col_index = lax.axis_index("col")
    core = col_index % CORE
    block_count = cols_dev * lax.axis_size("col") // BLK
    row_blocks = rows_dev // BLK
    listed = jnp.any(
        pattern[:, :, None] == jnp.arange(block_count, dtype=jnp.int32)[None, None, :], axis=1
    ).astype(jnp.float32)
    block_live = jnp.maximum(listed, listed.T)
    my_rows = lax.dynamic_slice_in_dim(block_live, row_number * row_blocks, row_blocks, 0)
    chip = lax.dynamic_slice_in_dim(my_rows, col_index - core, CORE, 1)
    tile_live = jnp.where(core == 0, chip[:, 0], chip[:, 1])
    tile_mask = jnp.repeat(tile_live, BLK)[:, None]
    live = chip.reshape(-1)
    global_rows = row_number * rows_dev + jnp.arange(rows_dev, dtype=jnp.int32)
    global_cols = col_index * cols_dev + jnp.arange(cols_dev, dtype=jnp.int32)
    identity = (global_rows[:, None] == global_cols[None, :]).astype(jnp.float32)
    current = 0.5 * identity + 0.45 / jnp.sqrt(jnp.float32(2 * NNZ * BLK)) * tile_mask * density
    where = jnp.concatenate(
        [col_places(col_index), row_places(row_number), core[None]]
    ).astype(jnp.int32)

    def purify(_, current):
        left = gather_cols(current)
        pair, left[1] = lax.optimization_barrier((to_pair(current, core), left[1]))
        right = gather_rows(pair)
        kept, given = call(
            square_body, where, live, left, right, [], (rows_dev // CORE, CORE * BLK)
        )
        square = gather_rows(kept + send(given, TWIN))
        keep, give = call(
            step_body, where, live, left, square, [kept, given], (rows_dev, BLK)
        )
        return keep + send(give, TWIN)

    return lax.fori_loop(0, ITERS, purify, current)


def solution(mesh):
    return jax.shard_map(
        local,
        mesh=mesh,
        in_specs=(P("row", "col"), P()),
        out_specs=P("row", "col"),
        check_vma=False,
    )
```
